256 devices in a mesh: fsdp: 32 (over z, y_hi, core), dp: 8 (over y_lo, x).
Axes of the slice: x: 4, y: 4 (y_hi: 2, y_lo: 2; y = y_hi * 2 + y_lo), z: 8, core: 2. Of those that a mesh axis runs over, the one named last changes fastest.
Arguments:
- features: bfloat16 [256, 16, 16, 640], P(('fsdp', 'dp')), may hold values from -100 to 100
- weight: bfloat16 [640, 5760], P('fsdp'), may hold values from -0.078125 to 0.078125
- group_norm_gain: float32 [640], replicated, may hold values from 0.1 to 1.9
- group_norm_shift: float32 [640], replicated, may hold values from -3 to 3
- conv_bias: float32 [640], replicated, may hold values from -3 to 3
- cotangent: bfloat16 [256, 16, 16, 640], P(('fsdp', 'dp')), may hold values from -6 to 6
Outputs:
- output: bfloat16 [256, 16, 16, 640], P(('fsdp', 'dp'))
- feature_gradient: bfloat16 [256, 16, 16, 640], P(('fsdp', 'dp'))
- weight_grad: float32 [640, 5760], P('fsdp')
- gain_gradient: float32 [640], replicated
- shift_grad: float32 [640], replicated
- bias_grad: float32 [640], replicated
The draws below stay inside these ranges and needn't reach their ends.
All inputs are finite; a program needn't handle non-finite values.
Results may differ from the reference program's by a relative error of at most 0.0044.
Values may be sent and summed in bfloat16 or wider, within the bound.
A program may use at most 128 MiB of HBM per device.

```python
import math
import jax
import jax.numpy as jnp
from jax import lax

CIN = 640
COUT = 640
GSIZE = 40
SIDE = 16
IMG_DEV = 1
IMAGE_COUNT = 256


def draw_features(key, part):
    key_base, key_chan, key_pix = jax.random.split(key, 3)
    full_shape = (IMAGE_COUNT, SIDE, SIDE, CIN)
    chan_scale = jnp.exp(jax.random.uniform(key_chan, (IMAGE_COUNT, 1, 1, CIN), jnp.float32, 0.0, math.log(10.0)))
    pix_scale = jnp.exp(jax.random.uniform(key_pix, (IMAGE_COUNT, SIDE, SIDE, 1), jnp.float32, 0.0, math.log(10.0)))
    base_draw = jnp.clip(jax.random.normal(key_base, full_shape, jnp.float32), -4.0, 4.0)
    return (base_draw * chan_scale * pix_scale / 4.0).astype(jnp.bfloat16)


def shard_levels(own_key, shape, shards, low, high):
    def one(position, shards_of):
        heights = jax.random.uniform(jax.random.fold_in(jax.random.fold_in(own_key, 6), position), (shards_of,), jnp.float32, low / len(shards), high / len(shards))
        return jnp.repeat(jnp.exp(heights), shape[position] // shards_of).reshape((-1,) + (1,) * (len(shape) - position - 1))

    loudness = one(*shards[0])
    for cut in shards[1:]:
        loudness = loudness * one(*cut)
    return loudness


def scatter_about(stream_key, dims, deviation, most, pieces=(), dtype=jnp.bfloat16):
    entries = jax.random.normal(stream_key, dims, jnp.float32) * deviation
    if len(pieces) > 0:
        entries = shard_levels(stream_key, dims, pieces, -0.22, 0.18) * entries
    return jnp.clip(entries, min=-most, max=most).astype(dtype)


def setup_inputs(seed: int = 0) -> dict:
    key_of = jax.random.split(jax.random.key(seed), 7)
    return {
        "features": draw_features(jax.random.fold_in(key_of[6], 71), 0),
        "weight": scatter_about(key_of[1], (CIN, 9 * COUT), (9 * CIN) ** -0.5, 0.078125, ((0, 32),)),
        "group_norm_gain": jnp.clip(1.0 + 0.18 * jax.random.normal(key_of[2], (CIN,), jnp.float32), 0.1, 1.9),
        "group_norm_shift": scatter_about(key_of[3], (CIN,), 0.5, 3.0, (), jnp.float32),
        "conv_bias": scatter_about(key_of[4], (COUT,), 0.5, 3.0, (), jnp.float32),
        "cotangent": scatter_about(key_of[5], (IMAGE_COUNT, SIDE, SIDE, COUT), 1.0, 6.0, ((0, 256),)),
    }


epsilon = 1e-05

def group_average(values):
    leading = values.shape[0]
    grouped = lax.optimization_barrier(jnp.sum(values.reshape(leading, -1, GSIZE), axis=2))
    return jnp.repeat(grouped, GSIZE, axis=1)

def apply_group_norm(features):
    widened = features.astype(jnp.float32)
    entry_count = features.shape[1] * features.shape[2] * GSIZE
    average = group_average(lax.optimization_barrier(jnp.sum(widened, axis=(1, 2)))) / entry_count
    centred = widened - average[:, None, None, :]
    spread = group_average(lax.optimization_barrier(jnp.sum(centred * centred, axis=(1, 2)))) / entry_count
    inverse_deviation = lax.rsqrt(spread + epsilon)
    return (centred * inverse_deviation[:, None, None, :], inverse_deviation, entry_count)

def spatial_pad(values):
    return jnp.pad(values, ((0, 0), (1, 1), (1, 1), (0, 0)))

def forward_conv(hidden, weight):
    padded = spatial_pad(hidden)
    running = jnp.zeros((IMAGE_COUNT * SIDE * SIDE, COUT), jnp.float32)
    for tap_index in range(9):
        row_off, col_off = divmod(tap_index, 3)
        window = padded[:, row_off:row_off + SIDE, col_off:col_off + SIDE, :].reshape(-1, CIN)
        running = running + jnp.dot(window, weight[:, tap_index * COUT:(tap_index + 1) * COUT], preferred_element_type=jnp.float32)
    return running.reshape(IMAGE_COUNT, SIDE, SIDE, COUT)

def backward_conv(cotangent, weight):
    padded = spatial_pad(cotangent)
    running = jnp.zeros((IMAGE_COUNT * SIDE * SIDE, CIN), jnp.float32)
    for tap_index in range(9):
        row_off, col_off = divmod(tap_index, 3)
        window = padded[:, 2 - row_off:2 - row_off + SIDE, 2 - col_off:2 - col_off + SIDE, :].reshape(-1, COUT)
        running = running + jnp.dot(window, weight[:, tap_index * COUT:(tap_index + 1) * COUT].T, preferred_element_type=jnp.float32)
    return running.reshape(IMAGE_COUNT, SIDE, SIDE, CIN)

def weight_terms(hidden, cotangent):
    padded = spatial_pad(hidden)
    groups = IMAGE_COUNT // IMG_DEV
    padded_groups = padded.reshape(groups, IMG_DEV, SIDE + 2, SIDE + 2, CIN)
    grad_groups = cotangent.reshape(groups, IMG_DEV * SIDE * SIDE, COUT)

    def one_group(running, pair_in):
        padded_one, grad_one = pair_in
        columns = []
        for tap_index in range(9):
            row_off, col_off = divmod(tap_index, 3)
            window = padded_one[:, row_off:row_off + SIDE, col_off:col_off + SIDE, :].reshape(-1, CIN)
            columns.append(jnp.dot(window.T, grad_one, preferred_element_type=jnp.float32))
        return (running + jnp.concatenate(columns, axis=1), jnp.float32(0.0))
    running, unused = lax.scan(one_group, jnp.zeros((CIN, 9 * COUT), jnp.float32), (padded_groups, grad_groups))
    return running

def reference(features, weight, group_norm_gain, group_norm_shift, conv_bias, cotangent):
    normalized_input, inverse_deviation, entry_count = apply_group_norm(features)
    preactivation = normalized_input * group_norm_gain + group_norm_shift
    hidden = jax.nn.silu(preactivation).astype(jnp.bfloat16)
    output = (forward_conv(hidden, weight) + conv_bias).astype(jnp.bfloat16)
    grad_hidden = backward_conv(cotangent, weight)
    sigmoid = jax.nn.sigmoid(preactivation)
    preactivation_gradient = grad_hidden * sigmoid * (1.0 + preactivation * (1.0 - sigmoid))
    norm_gradient = preactivation_gradient * group_norm_gain
    first_moment = group_average(lax.optimization_barrier(jnp.sum(norm_gradient, axis=(1, 2)))) / entry_count
    second_moment = group_average(lax.optimization_barrier(jnp.sum(norm_gradient * normalized_input, axis=(1, 2)))) / entry_count
    feature_gradient = ((norm_gradient - first_moment[:, None, None, :] - normalized_input * second_moment[:, None, None, :]) * inverse_deviation[:, None, None, :]).astype(jnp.bfloat16)
    weight_grad = weight_terms(hidden, cotangent) / IMAGE_COUNT
    gain_gradient = lax.optimization_barrier(jnp.sum(preactivation_gradient * normalized_input, axis=(0, 1, 2))) / IMAGE_COUNT
    shift_grad = lax.optimization_barrier(jnp.sum(preactivation_gradient, axis=(0, 1, 2))) / IMAGE_COUNT
    bias_grad = lax.optimization_barrier(jnp.sum(cotangent.astype(jnp.float32), axis=(0, 1, 2))) / IMAGE_COUNT
    return (output, feature_gradient, weight_grad, gain_gradient, shift_grad, bias_grad)
```

```python
import jax
import jax.numpy as jnp
from jax import lax
from jax.sharding import PartitionSpec as P

GSIZE = 40


epsilon = 1e-05


def group_average(values):
    leading = values.shape[0]
    grouped = jnp.sum(values.reshape(leading, -1, GSIZE), axis=2)
    return jnp.repeat(grouped, GSIZE, axis=1)


def apply_group_norm(features):
    widened = features.astype(jnp.float32)
    entry_count = features.shape[1] * features.shape[2] * GSIZE
    average = group_average(jnp.sum(widened, axis=(1, 2))) / entry_count
    centred = widened - average[:, None, None, :]
    spread = group_average(jnp.sum(centred * centred, axis=(1, 2))) / entry_count
    inverse_deviation = lax.rsqrt(spread + epsilon)
    return (centred * inverse_deviation[:, None, None, :], inverse_deviation, entry_count)


def spatial_pad(values):
    return jnp.pad(values, ((0, 0), (1, 1), (1, 1), (0, 0)))


def tap_window(padded, tap_index, side_len, flipped):
    row_off, col_off = divmod(tap_index, 3)
    if flipped:
        row_off, col_off = (2 - row_off, 2 - col_off)
    return padded[:, row_off : row_off + side_len, col_off : col_off + side_len, :]


def local(features, weight, group_norm_gain, group_norm_shift, conv_bias, cotangent):
    local_images = features.shape[0]
    side_len = features.shape[1]
    width_in = features.shape[3]
    width_out = cotangent.shape[3]
    images = local_images * lax.axis_size("fsdp") * lax.axis_size("dp")
    normalized_input, inverse_deviation, entry_count = apply_group_norm(features)
    preactivation = normalized_input * group_norm_gain + group_norm_shift
    hidden = jax.nn.silu(preactivation).astype(jnp.bfloat16)
    hidden_pad = spatial_pad(hidden)
    grad_pad = spatial_pad(cotangent)
    full_weight = lax.all_gather(weight, "fsdp", axis=0, tiled=True)
    conv_out = jnp.zeros((local_images, side_len, side_len, width_out), jnp.float32)
    for tap_index in range(9):
        conv_out = conv_out + jnp.einsum(
            "nijc,co->nijo",
            tap_window(hidden_pad, tap_index, side_len, False),
            full_weight[:, tap_index * width_out : (tap_index + 1) * width_out],
            preferred_element_type=jnp.float32,
        )
    output = (conv_out + conv_bias).astype(jnp.bfloat16)
    back_weight = lax.all_gather(weight, "fsdp", axis=0, tiled=True)
    grad_hidden = jnp.zeros((local_images, side_len, side_len, width_in), jnp.float32)
    for tap_index in range(9):
        grad_hidden = grad_hidden + jnp.einsum(
            "nijo,co->nijc",
            tap_window(grad_pad, tap_index, side_len, True),
            back_weight[:, tap_index * width_out : (tap_index + 1) * width_out],
            preferred_element_type=jnp.float32,
        )
    columns = []
    for tap_index in range(9):
        columns.append(
            jnp.einsum(
                "nijc,nijo->co",
                tap_window(hidden_pad, tap_index, side_len, False),
                cotangent,
                preferred_element_type=jnp.float32,
            )
        )
    local_term = jnp.concatenate(columns, axis=1)
    local_term = local_term.reshape(lax.axis_size("fsdp"), -1, 9 * width_out)
    weight_sum = lax.psum_scatter(local_term, "fsdp", scatter_dimension=0)
    weight_total = lax.psum(weight_sum.astype(jnp.float32), "dp")
    weight_grad = weight_total / images
    sigmoid = jax.nn.sigmoid(preactivation)
    preactivation_gradient = grad_hidden * sigmoid * (1.0 + preactivation * (1.0 - sigmoid))
    norm_gradient = preactivation_gradient * group_norm_gain
    first_moment = group_average(jnp.sum(norm_gradient, axis=(1, 2))) / entry_count
    second_moment = (
        group_average(jnp.sum(norm_gradient * normalized_input, axis=(1, 2))) / entry_count
    )
    feature_gradient = (
        (
            norm_gradient
            - first_moment[:, None, None, :]
            - normalized_input * second_moment[:, None, None, :]
        )
        * inverse_deviation[:, None, None, :]
    ).astype(jnp.bfloat16)
    gain_product = jnp.sum(preactivation_gradient * normalized_input, axis=(0, 1, 2))
    shift_term = jnp.sum(preactivation_gradient, axis=(0, 1, 2))
    bias_term = jnp.sum(cotangent.astype(jnp.float32), axis=(0, 1, 2))
    gain_total, shift_total, bias_total = lax.psum(
        (gain_product, shift_term, bias_term), ("fsdp", "dp")
    )
    return (
        output,
        feature_gradient,
        weight_grad,
        gain_total / images,
        shift_total / images,
        bias_total / images,
    )


def solution(mesh):
    in_specs = (
        P(("fsdp", "dp"), None, None, None),
        P("fsdp", None),
        P(),
        P(),
        P(),
        P(("fsdp", "dp"), None, None, None),
    )
    out_specs = (
        P(("fsdp", "dp"), None, None, None),
        P(("fsdp", "dp"), None, None, None),
        P("fsdp", None),
        P(),
        P(),
        P(),
    )
    return jax.shard_map(local, mesh=mesh, in_specs=in_specs, out_specs=out_specs, check_vma=False)
```

```python
import functools

import jax
import jax.numpy as jnp
import numpy as np
from jax import lax
from jax.experimental import pallas as pl
from jax.experimental.pallas import tpu as pltpu
from jax.sharding import PartitionSpec as P

MESH = pl.DeviceIdType.MESH
F32 = jnp.float32
BF16 = jnp.bfloat16
EPS = 1e-05
C = 640
GROUP = 40
SIDE = 16
PIX = SIDE * SIDE
CH = 384
NZ = 8
BLK = 320
ENTRIES = float(PIX * GROUP)
IMAGES = 256.0

ZW, AGB, AGA, RSA, RSB, SIB, SW, PC, FIN, V1, V2, V3, NSEM = (
    0, 16, 22, 28, 34, 40, 42, 50, 58, 74, 90, 94, 98)


def kernel(feat, w, par, cot, perm, ind, indt, out, fg, wg, vec,
           zbuf, mf, wall, term, xs, ds, hb, ht, cc, cb, pbuf, gh,
           o1, r1, ub, o2, r2, vb, cr, f2, rf, vs, v1, v2, v3, ss, rs):
    fi = lax.axis_index("fsdp")
    di = lax.axis_index("dp")
    z = fi // 4
    h = (fi // 2) % 2
    s = fi % 2
    lo = di // 4
    x = di % 4
    y = h * 2 + lo
    ra = (1 - s) * x + s * y
    rb = (1 - s) * y + s * x

    def dev(xx, yy, zz, sc):
        return {"fsdp": (zz * 2 + yy // 2) * 2 + sc, "dp": (yy % 2) * 4 + xx}

    def rc(src, dst, i, device):
        return pltpu.make_async_remote_copy(
            src_ref=src, dst_ref=dst, send_sem=ss.at[i], recv_sem=rs.at[i],
            device_id=device, device_id_type=MESH)

    sib = dev(x, y, z, 1 - s)
    a_right = dev((x + 1 - s) % 4, (y + s) % 4, z, s)
    a_left = dev((x + 3 * (1 - s)) % 4, (y + 3 * s) % 4, z, s)
    b_right = dev((x + s) % 4, (y + 1 - s) % 4, z, s)
    b_left = dev((x + 3 * s) % 4, (y + 3 * (1 - s)) % 4, z, s)
    zpeers = [(dz, dc) for dz in range(NZ) for dc in range(2) if (dz, dc) != (0, 0)]
    fpeers = [(dl, dx, dc) for dl in range(2) for dx in range(4) for dc in range(2)
              if (dl, dx, dc) != (0, 0, 0)]

    def zdev(dz, dc):
        return dev(x, y, (z + dz) % NZ, (s + dc) % 2)

    def fdev(dl, dx, dc):
        return dev((x + dx) % 4, h * 2 + (lo + dl) % 2, z, (s + dc) % 2)

    barrier = pltpu.get_barrier_semaphore()
    everyone = [zdev(*p) for p in zpeers] + [fdev(*p) for p in fpeers]
    everyone += [dev(x, (y + k) % 4, z, s) for k in (1, 2, 3)]
    for device in everyone:
        pl.semaphore_signal(barrier, inc=1, device_id=device, device_id_type=MESH)
    pl.semaphore_wait(barrier, len(everyone))

    def wcols(sc):
        k = jnp.minimum(sc * 8 + lo * 4 + x, 14)
        return w.at[:, pl.ds(pl.multiple_of(k * CH, CH), CH)]

    zc = []
    for dz, dc in zpeers:
        cp = rc(wcols((s + dc) % 2), zbuf.at[z * 2 + s], ZW + dz * 2 + dc, zdev(dz, dc))
        cp.start()
        zc.append(cp)
    own = pltpu.make_async_copy(wcols(s), zbuf.at[z * 2 + s], ss.at[ZW])
    own.start()

    pj = lax.broadcasted_iota(jnp.int32, (PIX, C), 0) % SIDE
    first, last = pj == 0, pj == SIDE - 1
    ct = cot[...].astype(F32)
    vs[2] = jnp.sum(ct, axis=0, keepdims=True) * jnp.ones((8, 1), F32)
    zero16 = jnp.zeros((SIDE, C), BF16)
    for b in range(3):
        cb[b, 0:SIDE, :] = zero16
        cb[b, SIDE + PIX:, :] = zero16
    cb[1, SIDE:SIDE + PIX, :] = cot[...]
    cb[2, SIDE:SIDE + PIX, :] = jnp.where(first, 0.0, pltpu.roll(ct, 1, 0)).astype(BF16)
    cb[0, SIDE:SIDE + PIX, :] = jnp.where(last, 0.0, pltpu.roll(ct, PIX - 1, 0)).astype(BF16)
    for tile in range(45):
        t, ot = divmod(tile, 5)
        a, b = divmod(t, 3)
        k, i = divmod(tile, 3)
        cc[k, 0:PIX, i * 128:(i + 1) * 128] = cb[
            b, SIDE * (2 - a):SIDE * (2 - a) + PIX, ot * 128:(ot + 1) * 128]
    cc[15, 0:PIX, :] = jnp.zeros((PIX, CH), BF16)
    theirs = pl.ds((1 - s) * 8, 8)
    sib_c = rc(cc.at[theirs, pl.ds(0, PIX)], cc.at[theirs, pl.ds(PIX, PIX)], SIB, sib)
    sib_c.start()

    def grouped(row):
        rows = jnp.broadcast_to(row, (8, C))
        small = jnp.dot(rows, ind[...], precision=lax.Precision.HIGHEST, preferred_element_type=F32)
        return jnp.dot(small, indt[...], precision=lax.Precision.HIGHEST,
                       preferred_element_type=F32)[0:1] / ENTRIES

    gain, shift, bias = par[0:1, :], par[1:2, :], par[2:3, :]
    xs[...] = jnp.dot(feat[...], perm[...], preferred_element_type=F32)
    mu = grouped(jnp.sum(xs[...], axis=0, keepdims=True))
    centred = xs[...] - mu
    xs[...] = centred
    inverse = lax.rsqrt(grouped(jnp.sum(centred * centred, axis=0, keepdims=True)) + EPS)
    xhat = xs[...] * inverse
    xs[...] = xhat
    pre = xhat * gain + shift
    sg = 1.0 / (1.0 + jnp.exp(-pre))
    ds[...] = sg * (1.0 + pre * (1.0 - sg))
    hid = pre * sg
    hb[...] = hid.astype(BF16)
    ht[:, 0:PIX] = hid.T.astype(BF16)
    sib_h = rc(ht.at[:, pl.ds(0, PIX)], ht.at[:, pl.ds(PIX, PIX)], SIB + 1, sib)
    sib_h.start()

    own.wait()
    for cp in zc:
        cp.wait_recv()
    for q in range(16):
        mf[q * 20:(q + 1) * 20, :] = zbuf[q].astype(F32)
    me = s * 16 + ra * 4 + rb
    wall[me] = mf[...].astype(BF16)

    def ring_gather(pos, right, left, piece, base):
        rt, lf = (pos + 1) % 4, (pos + 3) % 4
        first_sends = [
            rc(piece(pos, 0), piece(pos, 0), base, right),
            rc(piece(pos, 1), piece(pos, 1), base + 1, left),
            rc(piece(pos, 1), piece(pos, 1), base + 2, right),
            rc(piece(pos, 0), piece(pos, 0), base + 3, left),
        ]
        for cp in first_sends:
            cp.start()

        def relay(arrived):
            first_sends[0].wait_recv()
            f0 = rc(piece(lf, 0), piece(lf, 0), base + 4, right)
            f0.start()
            first_sends[1].wait_recv()
            f1 = rc(piece(rt, 1), piece(rt, 1), base + 5, left)
            f1.start()
            arrived(lf, 0, 1)
            arrived(rt, 1, 2)

            def finish():
                first_sends[2].wait_recv()
                arrived(lf, 1, 1)
                first_sends[3].wait_recv()
                arrived(rt, 0, 2)
                opp = (pos + 2) % 4
                f0.wait_recv()
                arrived(opp, 0, 3)
                f1.wait_recv()
                arrived(opp, 1, 3)
                for cp in first_sends + [f0, f1]:
                    cp.wait_send()
            return finish
        return relay

    def piece_b(j, half):
        return wall.at[s * 16 + ra * 4 + j, pl.ds(half * 160, 160)]

    def piece_a(j, half):
        return wall.at[pl.ds(s * 16 + j * 4 + half * 2, 2)]

    relay_b = ring_gather(rb, b_right, b_left, piece_b, AGB)

    sib_c.wait_recv()
    sib_h.wait_recv()

    def wgrad(i):
        res = jnp.dot(ht[...], cc[s * 8 + i], preferred_element_type=F32).astype(BF16)
        l2, xx = i // 4, i % 4
        for hh in range(2):
            yy = hh * 2 + l2
            idx = (1 - s) * (xx * 4 + yy) + s * (yy * 4 + xx)
            term[idx] = res[hh * BLK:(hh + 1) * BLK]

    pl.loop(0, 3)(wgrad)
    finish_b = relay_b(lambda j, half, rel: None)
    pl.loop(3, 5)(wgrad)
    finish_b()

    sib_w = []

    def to_sibling(j, half, rel):
        cp = rc(piece_a(j, half), piece_a(j, half), SW + rel * 2 + half, sib)
        cp.start()
        sib_w.append(cp)

    relay_a = ring_gather(ra, a_right, a_left, piece_a, AGA)
    to_sibling(ra, 0, 0)
    to_sibling(ra, 1, 0)
    pl.loop(5, 8)(wgrad)

    def ring_reduce(pos, right, left, piece, o, r, base, add):
        rt, lf, opp = (pos + 1) % 4, (pos + 3) % 4, (pos + 2) % 4
        sends = [
            rc(piece(opp, 0), o(0), base, right),
            rc(piece(opp, 1), o(1), base + 1, left),
            rc(piece(rt, 1), r(0, 1), base + 2, right),
            rc(piece(lf, 0), r(1, 0), base + 3, left),
        ]
        for cp in sends:
            cp.start()

        def middle():
            sends[0].wait_recv()
            add(rt, 0)
            g0 = rc(piece(rt, 0), r(0, 0), base + 4, right)
            g0.start()
            sends[1].wait_recv()
            add(lf, 1)
            g1 = rc(piece(lf, 1), r(1, 1), base + 5, left)
            g1.start()

            def finish():
                for cp in (sends[2], sends[3], g0, g1):
                    cp.wait_recv()
                for cp in sends + [g0, g1]:
                    cp.wait_send()
            return finish
        return middle

    def add_a(j, half):
        @pl.loop(0, 2)
        def _(q):
            at = j * 4 + half * 2 + q
            term[at] = (term[at].astype(F32) + o1[half * 2 + q].astype(F32)).astype(BF16)

    middle_ra = ring_reduce(
        ra, a_right, a_left,
        lambda j, half: term.at[pl.ds(j * 4 + half * 2, 2)],
        lambda half: o1.at[pl.ds(half * 2, 2)],
        lambda side, half: r1.at[side, pl.ds(half * 2, 2)],
        RSA, add_a)

    finish_a = relay_a(to_sibling)
    finish_a()
    finish_ra = middle_ra()

    gh[...] = jnp.zeros((PIX, C), F32)

    def conv(sc, i):
        l2, xx = i // 4, i % 4
        rows = []
        for hh in range(2):
            yy = hh * 2 + l2
            rows.append(wall[sc * 16 + (1 - sc) * (xx * 4 + yy) + sc * (yy * 4 + xx)])
        wk = jnp.concatenate(rows, axis=0)
        k = sc * 8 + i
        pbuf[k] = jnp.dot(hb[...], wk, preferred_element_type=F32)
        gh[...] += lax.dot_general(cc[k, 0:PIX], wk, (((1,), (1,)), ((), ())),
                                   preferred_element_type=F32)

    pl.loop(0, 8)(functools.partial(conv, s))
    for cp in sib_w:
        cp.wait_recv()
    pl.loop(0, 8)(functools.partial(conv, 1 - s))

    gp = gh[...] * ds[...]
    gh[...] = gp
    shift_sum = jnp.sum(gp, axis=0, keepdims=True)
    gain_sum = jnp.sum(gp * xs[...], axis=0, keepdims=True)
    vs[0] = jnp.broadcast_to(gain_sum, (8, C))
    vs[1] = jnp.broadcast_to(shift_sum, (8, C))
    row = lax.broadcasted_iota(jnp.int32, (8, C), 0)
    vs[3] = jnp.where(row == 0, vs[0], jnp.where(row == 1, vs[1], vs[2]))
    v1[z * 2 + s] = vs[3]
    vc = []
    for dz, dc in zpeers:
        cp = rc(vs.at[3], v1.at[z * 2 + s], V1 + dz * 2 + dc, zdev(dz, dc))
        cp.start()
        vc.append(cp)
    m1 = grouped(shift_sum * gain)
    m2 = grouped(gain_sum * gain)
    g = gh[...] * gain
    fgp = ((g - m1 - xs[...] * m2) * inverse).astype(BF16)
    fg[...] = lax.dot_general(fgp, perm[...], (((1,), (1,)), ((), ())),
                              preferred_element_type=F32).astype(BF16)

    finish_ra()
    for j in range(4):
        ub[j] = (term[ra * 4 + j].astype(F32) + r1[0, j].astype(F32)
                 + r1[1, j].astype(F32)).astype(BF16)

    def add_b(j, half):
        part = pl.ds(half * 160, 160)
        ub[j, part] = (ub[j, part].astype(F32) + o2[half].astype(F32)).astype(BF16)

    middle_rb = ring_reduce(
        rb, b_right, b_left,
        lambda j, half: ub.at[j, pl.ds(half * 160, 160)],
        lambda half: o2.at[half],
        lambda side, half: r2.at[side, pl.ds(half * 160, 160)],
        RSB, add_b)

    for cp in vc:
        cp.wait_recv()
    vs[4] = jnp.sum(v1[...], axis=0)
    v2[x] = vs[4]
    vx = []
    for k in (1, 2, 3):
        cp = rc(vs.at[4], v2.at[x], V2 + k, dev((x + k) % 4, y, z, s))
        cp.start()
        vx.append(cp)
    finish_rb = middle_rb()

    for ot in range(5):
        total = None
        for b in range(3):
            parts = []
            for a in range(3):
                k, i = divmod(5 * (3 * a + b) + ot, 3)
                p = pbuf[k, :, i * 128:(i + 1) * 128]
                pad = jnp.zeros((SIDE, 128), F32)
                if a == 0:
                    p = jnp.concatenate([pad, p[:PIX - SIDE]], axis=0)
                elif a == 2:
                    p = jnp.concatenate([p[SIDE:], pad], axis=0)
                parts.append(p)
            sb = parts[0] + parts[1] + parts[2]
            if b == 0:
                sb = jnp.where(first[:, :128], 0.0, pltpu.roll(sb, 1, 0))
            elif b == 2:
                sb = jnp.where(last[:, :128], 0.0, pltpu.roll(sb, PIX - 1, 0))
            total = sb if total is None else total + sb
        cols = slice(ot * 128, (ot + 1) * 128)
        out[:, cols] = (total + bias[:, cols]).astype(BF16)

    for cp in vx:
        cp.wait_recv()
    vs[5] = jnp.sum(v2[...], axis=0)
    v3[y] = vs[5]
    vy = []
    for k in (1, 2, 3):
        cp = rc(vs.at[5], v3.at[y], V3 + k, dev(x, (y + k) % 4, z, s))
        cp.start()
        vy.append(cp)

    finish_rb()
    total = ub[rb].astype(F32) + r2[0].astype(F32) + r2[1].astype(F32)
    for q in range(NZ):
        vb[q] = total[q * 40:(q + 1) * 40].astype(BF16)
    cr[z] = vb[z]
    pc = []
    for dz in range(1, NZ):
        cp = rc(vb.at[(z + dz) % NZ], cr.at[z], PC + dz, dev(x, y, (z + dz) % NZ, s))
        cp.start()
        pc.append(cp)
    for cp in vy:
        cp.wait_recv()
    vec[...] = jnp.sum(v3[...], axis=0) / IMAGES
    for cp in pc:
        cp.wait_recv()
    full = jnp.sum(cr[...].astype(F32), axis=0) / IMAGES
    f2[0] = full[0:20]
    f2[1] = full[20:40]
    slot = s * 8 + lo * 4 + x
    rf[slot] = f2[s]
    fc = []
    for dl, dx, dc in fpeers:
        cp = rc(f2.at[(s + dc) % 2], rf.at[slot], FIN + dl * 8 + dx * 2 + dc, fdev(dl, dx, dc))
        cp.start()
        fc.append(cp)
    for cp in fc:
        cp.wait_recv()
    for k in range(15):
        wg[:, k * CH:(k + 1) * CH] = rf[k]
    for cp in zc + [sib_c, sib_h] + sib_w + vc + vx + vy + pc + fc:
        cp.wait_send()


def local(features, weight, gain, shift, bias, cotangent):
    def to_inner(v):
        return v.reshape(NZ, 2, GROUP).transpose(1, 0, 2).reshape(C)

    def to_outer(v):
        return v.reshape(2, NZ, GROUP).transpose(1, 0, 2).reshape(C)

    par = jnp.stack([to_inner(gain), to_inner(shift), bias] + [bias] * 5)
    order = np.arange(C).reshape(NZ, 2, GROUP).transpose(1, 0, 2).reshape(C)
    perm = np.zeros((C, C), np.float32)
    perm[order, np.arange(C)] = 1.0
    ind = np.zeros((C, 128), np.float32)
    ind[np.arange(C), np.arange(C) // GROUP] = 1.0
    vm = pl.BlockSpec(memory_space=pltpu.VMEM)
    out, fg, wg, vec = pl.pallas_call(
        kernel,
        name="fused_step",
        out_shape=[
            jax.ShapeDtypeStruct((PIX, C), BF16),
            jax.ShapeDtypeStruct((PIX, C), BF16),
            jax.ShapeDtypeStruct((20, 9 * C), F32),
            jax.ShapeDtypeStruct((8, C), F32),
        ],
        in_specs=[vm] * 7,
        out_specs=[vm] * 4,
        scratch_shapes=[
            pltpu.VMEM((16, 20, CH), BF16),
            pltpu.VMEM((BLK, CH), F32),
            pltpu.VMEM((32, BLK, CH), BF16),
            pltpu.VMEM((16, BLK, CH), BF16),
            pltpu.VMEM((PIX, C), F32),
            pltpu.VMEM((PIX, C), F32),
            pltpu.VMEM((PIX, C), BF16),
            pltpu.VMEM((C, 2 * PIX), BF16),
            pltpu.VMEM((16, 2 * PIX, CH), BF16),
            pltpu.VMEM((3, PIX + 2 * SIDE, C), BF16),
            pltpu.VMEM((16, PIX, CH), F32),
            pltpu.VMEM((PIX, C), F32),
            pltpu.VMEM((4, BLK, CH), BF16),
            pltpu.VMEM((2, 4, BLK, CH), BF16),
            pltpu.VMEM((4, BLK, CH), BF16),
            pltpu.VMEM((2, 160, CH), BF16),
            pltpu.VMEM((2, BLK, CH), BF16),
            pltpu.VMEM((NZ, 40, CH), BF16),
            pltpu.VMEM((NZ, 40, CH), BF16),
            pltpu.VMEM((2, 20, CH), F32),
            pltpu.VMEM((16, 20, CH), F32),
            pltpu.VMEM((6, 8, C), F32),
            pltpu.VMEM((16, 8, C), F32),
            pltpu.VMEM((4, 8, C), F32),
            pltpu.VMEM((4, 8, C), F32),
            pltpu.SemaphoreType.DMA((NSEM,)),
            pltpu.SemaphoreType.DMA((NSEM,)),
        ],
        compiler_params=pltpu.CompilerParams(
            collective_id=0, has_side_effects=True, vmem_limit_bytes=60 * 1024 * 1024),
    )(features.reshape(PIX, C), weight, par, cotangent.reshape(PIX, C),
      jnp.asarray(perm, BF16), jnp.asarray(ind), jnp.asarray(ind.T.copy()))
    shape = features.shape
    return (out.reshape(shape), fg.reshape(shape), wg,
            to_outer(vec[0]), to_outer(vec[1]), vec[2])


def solution(mesh):
    img = P(("fsdp", "dp"), None, None, None)
    return jax.shard_map(
        local, mesh=mesh,
        in_specs=(img, P("fsdp", None), P(), P(), P(), img),
        out_specs=(img, img, P("fsdp", None), P(), P(), P()),
        check_vma=False)
```

```python
import functools

import jax
import jax.numpy as jnp
import numpy as np
from jax import lax
from jax.experimental import pallas as pl
from jax.experimental.pallas import tpu as pltpu
from jax.sharding import PartitionSpec as P

MESH = pl.DeviceIdType.MESH
F32 = jnp.float32
BF16 = jnp.bfloat16
EPS = 1e-05
C = 640
GROUP = 40
SIDE = 16
PIX = SIDE * SIDE
CH = 384
NZ = 8
BLK = 320
ENTRIES = float(PIX * GROUP)
IMAGES = 256.0

ZW, AGB, AGA, RSA, RSB, SIB, SW, PC, FIN, V1, V2, V3, NSEM = (
    0, 16, 22, 28, 34, 40, 42, 50, 58, 74, 90, 94, 98)


def kernel(feat, w, p_gain, p_shift, p_bias, cot, perm, ind, indt,
           out, fg, wg, out_gain, out_shift, out_bias,
           zbuf, mf, wall, term, xs, ds, hb, ht, cc, cb, pbuf, gh,
           o1, r1, ub, o2, r2, vb, cr, tf, f2, rf, vs, v1, v2, v3, scot, vo, ss, rs):
    fi = lax.axis_index("fsdp")
    di = lax.axis_index("dp")
    z = fi // 4
    h = (fi // 2) % 2
    s = fi % 2
    lo = di // 4
    x = di % 4
    y = h * 2 + lo
    ra = (1 - s) * x + s * y
    rb = (1 - s) * y + s * x

    def dev(xx, yy, zz, sc):
        return {"fsdp": (zz * 2 + yy // 2) * 2 + sc, "dp": (yy % 2) * 4 + xx}

    def rc(src, dst, i, device):
        return pltpu.make_async_remote_copy(
            src_ref=src, dst_ref=dst, send_sem=ss.at[i], recv_sem=rs.at[i],
            device_id=device, device_id_type=MESH)

    sib = dev(x, y, z, 1 - s)
    a_right = dev((x + 1 - s) % 4, (y + s) % 4, z, s)
    a_left = dev((x + 3 * (1 - s)) % 4, (y + 3 * s) % 4, z, s)
    b_right = dev((x + s) % 4, (y + 1 - s) % 4, z, s)
    b_left = dev((x + 3 * s) % 4, (y + 3 * (1 - s)) % 4, z, s)
    zpeers = [(dz, dc) for dz in range(NZ) for dc in range(2) if (dz, dc) != (0, 0)]
    fpeers = [(dl, dx, dc) for dl in range(2) for dx in range(4) for dc in range(2)
              if (dl, dx, dc) != (0, 0, 0)]

    def zdev(dz, dc):
        return dev(x, y, (z + dz) % NZ, (s + dc) % 2)

    def fdev(dl, dx, dc):
        return dev((x + dx) % 4, h * 2 + (lo + dl) % 2, z, (s + dc) % 2)

    barrier = pltpu.get_barrier_semaphore()
    everyone = [zdev(*p) for p in zpeers] + [fdev(*p) for p in fpeers]
    everyone += [dev(x, (y + k) % 4, z, s) for k in (1, 2, 3)]
    for device in everyone:
        pl.semaphore_signal(barrier, inc=1, device_id=device, device_id_type=MESH)

    pj = lax.broadcasted_iota(jnp.int32, (PIX, C), 0) % SIDE
    first, last = pj == 0, pj == SIDE - 1
    zero16 = jnp.zeros((SIDE, C), BF16)
    for b in range(3):
        cb[b, 0:SIDE, :] = zero16
        cb[b, SIDE + PIX:, :] = zero16

    def windows(source, at):
        wide = source[...].astype(F32)
        cb[1, SIDE:SIDE + PIX, :] = source[...]
        cb[2, SIDE:SIDE + PIX, :] = jnp.where(first, 0.0, pltpu.roll(wide, 1, 0)).astype(BF16)
        cb[0, SIDE:SIDE + PIX, :] = jnp.where(last, 0.0, pltpu.roll(wide, PIX - 1, 0)).astype(BF16)
        for tile in range(45):
            t, ot = divmod(tile, 5)
            a, b = divmod(t, 3)
            k, i = divmod(tile, 3)
            cc[k, at:at + PIX, i * 128:(i + 1) * 128] = cb[
                b, SIDE * (2 - a):SIDE * (2 - a) + PIX, ot * 128:(ot + 1) * 128]
        cc[15, at:at + PIX, :] = jnp.zeros((PIX, CH), BF16)
        return jnp.sum(wide, axis=0, keepdims=True)

    bias_sum = windows(cot, 0)
    for i in range(5):
        vs[0, 10 + i:11 + i, :] = bias_sum[:, i * 128:(i + 1) * 128]
    vs[0, 15:16, :] = jnp.zeros((1, 128), F32)
    pl.semaphore_wait(barrier, len(everyone))
    sib_c = rc(cot, scot, SIB, sib)
    sib_c.start()
    def wcols(sc):
        k = jnp.minimum(sc * 8 + lo * 4 + x, 14)
        return w.at[:, pl.ds(pl.multiple_of(k * CH, CH), CH)]

    zc = []
    for dz, dc in zpeers:
        cp = rc(wcols((s + dc) % 2), zbuf.at[z * 2 + s], ZW + dz * 2 + dc, zdev(dz, dc))
        cp.start()
        zc.append(cp)
    own = pltpu.make_async_copy(wcols(s), zbuf.at[z * 2 + s], ss.at[ZW])
    own.start()

    def grouped(row):
        rows = jnp.broadcast_to(row, (8, C))
        small = jnp.dot(rows, ind[...], precision=lax.Precision.HIGHEST, preferred_element_type=F32)
        return jnp.dot(small, indt[...], precision=lax.Precision.HIGHEST,
                       preferred_element_type=F32)[0:1] / ENTRIES

    def thirds(v):
        top = v.astype(BF16)
        rest = v - top.astype(F32)
        mid = rest.astype(BF16)
        return jnp.concatenate([top.astype(F32), mid.astype(F32), rest - mid.astype(F32)], axis=0).astype(BF16)

    def moved(v, side):
        parts = lax.dot_general(thirds(v), perm[...], (((1,), (side,)), ((), ())),
                                preferred_element_type=F32)
        return parts[0:8] + parts[8:16] + parts[16:24]

    bias = p_bias[...].reshape(1, C)
    row8 = lax.broadcasted_iota(jnp.int32, (8, C), 0)
    inner = moved(jnp.where(row8 == 0, p_gain[...].reshape(1, C), p_shift[...].reshape(1, C)), 0)
    gain, shift = inner[0:1], inner[1:2]
    xs[...] = jnp.dot(feat[...], perm[...], preferred_element_type=F32)
    mu = grouped(jnp.sum(xs[...], axis=0, keepdims=True))
    centred = xs[...] - mu
    xs[...] = centred
    inverse = lax.rsqrt(grouped(jnp.sum(centred * centred, axis=0, keepdims=True)) + EPS)
    xhat = xs[...] * inverse
    xs[...] = xhat
    pre = xhat * gain + shift
    sg = 1.0 / (1.0 + jnp.exp(-pre))
    ds[...] = sg * (1.0 + pre * (1.0 - sg))
    hid = pre * sg
    hb[...] = hid.astype(BF16)
    ht[:, 0:PIX] = hid.T.astype(BF16)
    def ring_gather(pos, right, left, piece, base):
        rt, lf = (pos + 1) % 4, (pos + 3) % 4
        first_sends = [
            rc(piece(pos, 0), piece(pos, 0), base, right),
            rc(piece(pos, 1), piece(pos, 1), base + 1, left),
            rc(piece(pos, 1), piece(pos, 1), base + 2, right),
            rc(piece(pos, 0), piece(pos, 0), base + 3, left),
        ]
        for cp in first_sends:
            cp.start()

        def relay(arrived):
            first_sends[0].wait_recv()
            f0 = rc(piece(lf, 0), piece(lf, 0), base + 4, right)
            f0.start()
            first_sends[1].wait_recv()
            f1 = rc(piece(rt, 1), piece(rt, 1), base + 5, left)
            f1.start()
            arrived(lf, 0, 1)
            arrived(rt, 1, 2)

            def sides():
                first_sends[2].wait_recv()
                arrived(lf, 1, 1)
                first_sends[3].wait_recv()
                arrived(rt, 0, 2)

            def finish():
                opp = (pos + 2) % 4
                f0.wait_recv()
                arrived(opp, 0, 3)
                f1.wait_recv()
                arrived(opp, 1, 3)
                for cp in first_sends + [f0, f1]:
                    cp.wait_send()
            return sides, finish
        return relay

    def piece_b(j, half):
        return wall.at[s * 16 + ra * 4 + j, pl.ds(half * 160, 160)]

    def piece_a(j, half):
        return wall.at[pl.ds(s * 16 + j * 4 + half * 2, 2)]


    sib_h = rc(ht.at[:, pl.ds(0, PIX)], ht.at[:, pl.ds(PIX, PIX)], SIB + 1, sib)
    sib_h.start()


    sib_c.wait_recv()
    windows(scot, PIX)
    sib_h.wait_recv()

    def chunk(sc, n, late):
        e = 1 - late
        l2 = (1 - sc) * (n % 2) + sc * ((lo + e) % 2)
        xx = (1 - sc) * ((x + e + 2 * (n // 2)) % 4) + sc * n
        return l2 * 4 + xx

    def wgrad(i):
        res = jnp.dot(ht[...], cc[s * 8 + i], preferred_element_type=F32).astype(BF16)
        l2, xx = i // 4, i % 4
        for hh in range(2):
            yy = hh * 2 + l2
            idx = (1 - s) * (xx * 4 + yy) + s * (yy * 4 + xx)
            term[idx] = res[hh * BLK:(hh + 1) * BLK]


    sib_w = {}

    def to_sibling(j, half, rel):
        cp = rc(piece_a(j, half), piece_a(j, half), SW + rel * 2 + half, sib)
        cp.start()
        sib_w[rel, half] = cp

    def ring_reduce(pos, right, left, piece, o, r, base, add, between=lambda: None):
        rt, lf, opp = (pos + 1) % 4, (pos + 3) % 4, (pos + 2) % 4
        sends = [
            rc(piece(opp, 0), o(0), base, right),
            rc(piece(opp, 1), o(1), base + 1, left),
            rc(piece(rt, 1), r(0, 1), base + 2, right),
            rc(piece(lf, 0), r(1, 0), base + 3, left),
        ]
        for cp in sends[:2]:
            cp.start()
        between()
        for cp in sends[2:]:
            cp.start()

        def middle():
            sends[0].wait_recv()
            add(rt, 0)
            g0 = rc(piece(rt, 0), r(0, 0), base + 4, right)
            g0.start()
            sends[1].wait_recv()
            add(lf, 1)
            g1 = rc(piece(lf, 1), r(1, 1), base + 5, left)
            g1.start()

            def finish():
                for cp in (sends[2], sends[3], g0, g1):
                    cp.wait_recv()
                for cp in sends + [g0, g1]:
                    cp.wait_send()
            return finish
        return middle

    def add_a(j, half):
        @pl.loop(0, 2)
        def _(q):
            at = j * 4 + half * 2 + q
            term[at] = (term[at].astype(F32) + o1[half * 2 + q].astype(F32)).astype(BF16)

    pl.loop(0, 4)(lambda n: wgrad(chunk(s, n, 1)))
    middle_ra = ring_reduce(
        ra, a_right, a_left,
        lambda j, half: term.at[pl.ds(j * 4 + half * 2, 2)],
        lambda half: o1.at[pl.ds(half * 2, 2)],
        lambda side, half: r1.at[side, pl.ds(half * 2, 2)],
        RSA, add_a, between=lambda: pl.loop(0, 4)(lambda n: wgrad(chunk(s, n, 0))))

    own.wait()
    for cp in zc:
        cp.wait_recv()
    for q in range(16):
        mf[q * 20:(q + 1) * 20, :] = zbuf[q].astype(F32)
    me = s * 16 + ra * 4 + rb
    wall[me] = mf[...].astype(BF16)

    relay_b = ring_gather(rb, b_right, b_left, piece_b, AGB)
    finish_ra = middle_ra()
    for step in relay_b(lambda j, half, rel: None):
        step()
    relay_a = ring_gather(ra, a_right, a_left, piece_a, AGA)
    to_sibling(ra, 0, 0)
    to_sibling(ra, 1, 0)

    finish_ra()

    def sum_a(j):
        return term[ra * 4 + j].astype(F32) + r1[0, j].astype(F32) + r1[1, j].astype(F32)

    @pl.loop(0, 4)
    def _(j):
        ub[j] = sum_a(j).astype(BF16)

    def add_b(j, half):
        part = pl.ds(half * 160, 160)
        ub[j, part] = (ub[j, part].astype(F32) + o2[half].astype(F32)).astype(BF16)

    middle_rb = ring_reduce(
        rb, b_right, b_left,
        lambda j, half: ub.at[j, pl.ds(half * 160, 160)],
        lambda half: o2.at[half],
        lambda side, half: r2.at[side, pl.ds(half * 160, 160)],
        RSB, add_b)
    sides_a, finish_a = relay_a(to_sibling)
    finish_rb = middle_rb()

    gh[...] = jnp.zeros((PIX, C), F32)

    def block(sc, i):
        l2, xx = i // 4, i % 4
        rows = []
        for hh in range(2):
            yy = hh * 2 + l2
            rows.append(wall[sc * 16 + (1 - sc) * (xx * 4 + yy) + sc * (yy * 4 + xx)])
        return jnp.concatenate(rows, axis=0)

    def back(sc, i):
        gh[...] += lax.dot_general(cc[sc * 8 + i, 0:PIX], block(sc, i), (((1,), (1,)), ((), ())),
                                   preferred_element_type=F32)

    def forth(sc, i):
        pbuf[sc * 8 + i] = jnp.dot(hb[...], block(sc, i), preferred_element_type=F32)

    def loop(f, sc, late):
        pl.loop(0, 4)(lambda n: f(sc, chunk(sc, n, late)))

    def both(sc, i):
        wk = block(sc, i)
        k = sc * 8 + i
        pbuf[k] = jnp.dot(hb[...], wk, preferred_element_type=F32)
        gh[...] += lax.dot_general(cc[k, 0:PIX], wk, (((1,), (1,)), ((), ())),
                                   preferred_element_type=F32)

    finish_rb()
    total = sum_a(rb) + r2[0].astype(F32) + r2[1].astype(F32)
    for q in range(NZ):
        tf[q] = total[q * 40:(q + 1) * 40]
        vb[q] = total[q * 40:(q + 1) * 40].astype(BF16)
    pc = []
    for dz in range(1, NZ):
        cp = rc(vb.at[(z + dz) % NZ], cr.at[z], PC + dz, dev(x, y, (z + dz) % NZ, s))
        cp.start()
        pc.append(cp)
    cr[z] = jnp.zeros((40, CH), BF16)

    sides_a()
    loop(both, s, 0)

    for cp in pc:
        cp.wait_recv()
    full = (jnp.sum(cr[...].astype(F32), axis=0) + tf[z]) / IMAGES
    f2[0] = full[0:20]
    f2[1] = full[20:40]
    slot = s * 8 + lo * 4 + x
    rf[slot] = f2[s]
    fc = []
    for dl, dx, dc in fpeers:
        cp = rc(f2.at[(s + dc) % 2], rf.at[slot], FIN + dl * 8 + dx * 2 + dc, fdev(dl, dx, dc))
        cp.start()
        fc.append(cp)

    for rel, half in ((1, 0), (2, 1), (1, 1), (2, 0)):
        sib_w[rel, half].wait_recv()
    loop(both, 1 - s, 0)
    finish_a()
    loop(back, s, 1)
    for rel, half in ((0, 0), (0, 1), (3, 0), (3, 1)):
        sib_w[rel, half].wait_recv()
    loop(back, 1 - s, 1)

    gp = gh[...] * ds[...]
    gh[...] = gp
    shift_sum = jnp.sum(gp, axis=0, keepdims=True)
    gain_sum = jnp.sum(gp * xs[...], axis=0, keepdims=True)
    for i in range(5):
        vs[0, i:i + 1, :] = gain_sum[:, i * 128:(i + 1) * 128]
        vs[0, 5 + i:6 + i, :] = shift_sum[:, i * 128:(i + 1) * 128]
    v1[z * 2 + s] = vs[0]
    vc = []
    for dz, dc in zpeers:
        cp = rc(vs.at[0], v1.at[z * 2 + s], V1 + dz * 2 + dc, zdev(dz, dc))
        cp.start()
        vc.append(cp)

    m1 = grouped(shift_sum * gain)
    m2 = grouped(gain_sum * gain)
    g = gh[...] * gain
    fgp = ((g - m1 - xs[...] * m2) * inverse).astype(BF16)
    fg[...] = lax.dot_general(fgp, perm[...], (((1,), (1,)), ((), ())),
                              preferred_element_type=F32).astype(BF16)

    for cp in vc:
        cp.wait_recv()
    vs[1] = jnp.sum(v1[...], axis=0)
    v2[x] = vs[1]
    vx = []
    for k in (1, 2, 3):
        cp = rc(vs.at[1], v2.at[x], V2 + k, dev((x + k) % 4, y, z, s))
        cp.start()
        vx.append(cp)
    loop(forth, s, 1)
    for cp in vx:
        cp.wait_recv()
    vs[2] = jnp.sum(v2[...], axis=0)
    v3[y] = vs[2]
    vy = []
    for k in (1, 2, 3):
        cp = rc(vs.at[2], v3.at[y], V3 + k, dev(x, (y + k) % 4, z, s))
        cp.start()
        vy.append(cp)
    loop(forth, 1 - s, 1)

    for ot in range(5):
        total = None
        for b in range(3):
            parts = []
            for a in range(3):
                k, i = divmod(5 * (3 * a + b) + ot, 3)
                p = pbuf[k, :, i * 128:(i + 1) * 128]
                pad = jnp.zeros((SIDE, 128), F32)
                if a == 0:
                    p = jnp.concatenate([pad, p[:PIX - SIDE]], axis=0)
                elif a == 2:
                    p = jnp.concatenate([p[SIDE:], pad], axis=0)
                parts.append(p)
            sb = parts[0] + parts[1] + parts[2]
            if b == 0:
                sb = jnp.where(first[:, :128], 0.0, pltpu.roll(sb, 1, 0))
            elif b == 2:
                sb = jnp.where(last[:, :128], 0.0, pltpu.roll(sb, PIX - 1, 0))
            total = sb if total is None else total + sb
        cols = slice(ot * 128, (ot + 1) * 128)
        out[:, cols] = (total + bias[:, cols]).astype(BF16)

    for cp in fc:
        cp.wait_recv()
    for k in range(15):
        wg[:, k * CH:(k + 1) * CH] = rf[k]
    for cp in vy:
        cp.wait_recv()
    sums = jnp.sum(v3[...], axis=0) / IMAGES
    vo[...] = jnp.zeros((8, C), F32)
    for q in range(3):
        for i in range(5):
            vo[q:q + 1, i * 128:(i + 1) * 128] = sums[q * 5 + i:q * 5 + i + 1]
    outer = moved(vo[...], 1)
    out_gain[...] = outer[0:1].reshape(C)
    out_shift[...] = outer[1:2].reshape(C)
    out_bias[...] = vo[2:3].reshape(C)
    for cp in zc + [sib_c, sib_h] + list(sib_w.values()) + vc + vx + vy + pc + fc:
        cp.wait_send()


def local(features, weight, gain, shift, bias, cotangent):
    order = np.arange(C).reshape(NZ, 2, GROUP).transpose(1, 0, 2).reshape(C)
    perm = np.zeros((C, C), np.float32)
    perm[order, np.arange(C)] = 1.0
    ind = np.zeros((C, 128), np.float32)
    ind[np.arange(C), np.arange(C) // GROUP] = 1.0
    vm = pl.BlockSpec(memory_space=pltpu.VMEM)
    out, fg, wg, g_gain, g_shift, g_bias = pl.pallas_call(
        kernel,
        name="fused_step",
        out_shape=[
            jax.ShapeDtypeStruct((PIX, C), BF16),
            jax.ShapeDtypeStruct((PIX, C), BF16),
            jax.ShapeDtypeStruct((20, 9 * C), F32),
            jax.ShapeDtypeStruct((C,), F32),
            jax.ShapeDtypeStruct((C,), F32),
            jax.ShapeDtypeStruct((C,), F32),
        ],
        in_specs=[vm] * 9,
        out_specs=[vm] * 6,
        scratch_shapes=[
            pltpu.VMEM((16, 20, CH), BF16),
            pltpu.VMEM((BLK, CH), F32),
            pltpu.VMEM((32, BLK, CH), BF16),
            pltpu.VMEM((16, BLK, CH), BF16),
            pltpu.VMEM((PIX, C), F32),
            pltpu.VMEM((PIX, C), F32),
            pltpu.VMEM((PIX, C), BF16),
            pltpu.VMEM((C, 2 * PIX), BF16),
            pltpu.VMEM((16, 2 * PIX, CH), BF16),
            pltpu.VMEM((3, PIX + 2 * SIDE, C), BF16),
            pltpu.VMEM((16, PIX, CH), F32),
            pltpu.VMEM((PIX, C), F32),
            pltpu.VMEM((4, BLK, CH), BF16),
            pltpu.VMEM((2, 4, BLK, CH), BF16),
            pltpu.VMEM((4, BLK, CH), BF16),
            pltpu.VMEM((2, 160, CH), BF16),
            pltpu.VMEM((2, BLK, CH), BF16),
            pltpu.VMEM((NZ, 40, CH), BF16),
            pltpu.VMEM((NZ, 40, CH), BF16),
            pltpu.VMEM((NZ, 40, CH), F32),
            pltpu.VMEM((2, 20, CH), F32),
            pltpu.VMEM((16, 20, CH), F32),
            pltpu.VMEM((3, 16, 128), F32),
            pltpu.VMEM((16, 16, 128), F32),
            pltpu.VMEM((4, 16, 128), F32),
            pltpu.VMEM((4, 16, 128), F32),
            pltpu.VMEM((PIX, C), BF16),
            pltpu.VMEM((8, C), F32),
            pltpu.SemaphoreType.DMA((NSEM,)),
            pltpu.SemaphoreType.DMA((NSEM,)),
        ],
        compiler_params=pltpu.CompilerParams(
            collective_id=0, has_side_effects=True, vmem_limit_bytes=60 * 1024 * 1024),
    )(features.reshape(PIX, C), weight, gain, shift, bias, cotangent.reshape(PIX, C),
      jnp.asarray(perm, BF16), jnp.asarray(ind), jnp.asarray(ind.T.copy()))
    shape = features.shape
    return out.reshape(shape), fg.reshape(shape), wg, g_gain, g_shift, g_bias


def solution(mesh):
    img = P(("fsdp", "dp"), None, None, None)
    return jax.shard_map(
        local, mesh=mesh,
        in_specs=(img, P("fsdp", None), P(), P(), P(), img),
        out_specs=(img, img, P("fsdp", None), P(), P(), P()),
        check_vma=False)
```

```python
import functools

import jax
import jax.numpy as jnp
import numpy as np
from jax import lax
from jax.experimental import pallas as pl
from jax.experimental.pallas import tpu as pltpu
from jax.sharding import PartitionSpec as P

MESH = pl.DeviceIdType.MESH
F32 = jnp.float32
BF16 = jnp.bfloat16
EPS = 1e-05
C = 640
GROUP = 40
SIDE = 16
PIX = SIDE * SIDE
CH = 384
NZ = 8
BLK = 320
ENTRIES = float(PIX * GROUP)
IMAGES = 256.0

ZW, AGB, AGA, RSA, RSB, SIB, SW, PC, FIN, V1, V2, V3, NSEM = (
    0, 16, 22, 28, 34, 40, 42, 50, 58, 74, 90, 94, 98)


def kernel(feat_in, w_in, p_gain_in, p_shift_in, p_bias_in, cot_in, perm_in, ind_in, indt_in,
           out, fg, wg, out_gain, out_shift, out_bias,
           zbuf, mf, wall, term, xs, ds, hb, ht, cc, cb, pbuf, gh,
           o1, r1, ub, o2, r2, vb, cr, tf, f2, rf, vs, v1, v2, v3, scot, vo,
           feat, w, p_gain, p_shift, p_bias, cot, perm, ind, indt, ls, ss, rs):
    fi = lax.axis_index("fsdp")
    di = lax.axis_index("dp")
    z = fi // 4
    h = (fi // 2) % 2
    s = fi % 2
    lo = di // 4
    x = di % 4
    y = h * 2 + lo
    ra = (1 - s) * x + s * y
    rb = (1 - s) * y + s * x

    def dev(xx, yy, zz, sc):
        return {"fsdp": (zz * 2 + yy // 2) * 2 + sc, "dp": (yy % 2) * 4 + xx}

    def rc(src, dst, i, device):
        return pltpu.make_async_remote_copy(
            src_ref=src, dst_ref=dst, send_sem=ss.at[i], recv_sem=rs.at[i],
            device_id=device, device_id_type=MESH)

    sib = dev(x, y, z, 1 - s)
    a_right = dev((x + 1 - s) % 4, (y + s) % 4, z, s)
    a_left = dev((x + 3 * (1 - s)) % 4, (y + 3 * s) % 4, z, s)
    b_right = dev((x + s) % 4, (y + 1 - s) % 4, z, s)
    b_left = dev((x + 3 * s) % 4, (y + 3 * (1 - s)) % 4, z, s)
    zpeers = [(dz, dc) for dz in range(NZ) for dc in range(2) if (dz, dc) != (0, 0)]
    fpeers = [(dl, dx, dc) for dl in range(2) for dx in range(4) for dc in range(2)
              if (dl, dx, dc) != (0, 0, 0)]

    def zdev(dz, dc):
        return dev(x, y, (z + dz) % NZ, (s + dc) % 2)

    def fdev(dl, dx, dc):
        return dev((x + dx) % 4, h * 2 + (lo + dl) % 2, z, (s + dc) % 2)

    barrier = pltpu.get_barrier_semaphore()
    everyone = [zdev(*p) for p in zpeers] + [fdev(*p) for p in fpeers]
    everyone += [dev(x, (y + k) % 4, z, s) for k in (1, 2, 3)]
    for device in everyone:
        pl.semaphore_signal(barrier, inc=1, device_id=device, device_id_type=MESH)

    pairs = [(cot_in, cot), (feat_in, feat), (perm_in, perm), (ind_in, ind), (indt_in, indt),
             (w_in, w), (p_gain_in, p_gain), (p_shift_in, p_shift), (p_bias_in, p_bias)]
    loads = [pltpu.make_async_copy(a, b, ls.at[i]) for i, (a, b) in enumerate(pairs)]
    for cp in loads:
        cp.start()

    pj = lax.broadcasted_iota(jnp.int32, (PIX, C), 0) % SIDE
    first, last = pj == 0, pj == SIDE - 1
    zero16 = jnp.zeros((SIDE, C), BF16)
    for b in range(3):
        cb[b, 0:SIDE, :] = zero16
        cb[b, SIDE + PIX:, :] = zero16

    def windows(source, at):
        wide = source[...].astype(F32)
        cb[1, SIDE:SIDE + PIX, :] = source[...]
        cb[2, SIDE:SIDE + PIX, :] = jnp.where(first, 0.0, pltpu.roll(wide, 1, 0)).astype(BF16)
        cb[0, SIDE:SIDE + PIX, :] = jnp.where(last, 0.0, pltpu.roll(wide, PIX - 1, 0)).astype(BF16)
        for tile in range(45):
            t, ot = divmod(tile, 5)
            a, b = divmod(t, 3)
            k, i = divmod(tile, 3)
            cc[k, at:at + PIX, i * 128:(i + 1) * 128] = cb[
                b, SIDE * (2 - a):SIDE * (2 - a) + PIX, ot * 128:(ot + 1) * 128]
        cc[15, at:at + PIX, :] = jnp.zeros((PIX, CH), BF16)
        return jnp.sum(wide, axis=0, keepdims=True)

    loads[0].wait()
    bias_sum = windows(cot, 0)
    for i in range(5):
        vs[0, 10 + i:11 + i, :] = bias_sum[:, i * 128:(i + 1) * 128]
    vs[0, 15:16, :] = jnp.zeros((1, 128), F32)
    def grouped(row):
        rows = jnp.broadcast_to(row, (8, C))
        small = jnp.dot(rows, ind[...], precision=lax.Precision.HIGHEST, preferred_element_type=F32)
        return jnp.dot(small, indt[...], precision=lax.Precision.HIGHEST,
                       preferred_element_type=F32)[0:1] / ENTRIES

    def thirds(v):
        top = v.astype(BF16)
        rest = v - top.astype(F32)
        mid = rest.astype(BF16)
        return jnp.concatenate([top.astype(F32), mid.astype(F32), rest - mid.astype(F32)], axis=0).astype(BF16)

    def moved(v, side):
        parts = lax.dot_general(thirds(v), perm[...], (((1,), (side,)), ((), ())),
                                preferred_element_type=F32)
        return parts[0:8] + parts[8:16] + parts[16:24]

    for cp in loads[1:]:
        cp.wait()
    bias = p_bias[...].reshape(1, C)
    row8 = lax.broadcasted_iota(jnp.int32, (8, C), 0)
    inner = moved(jnp.where(row8 == 0, p_gain[...].reshape(1, C), p_shift[...].reshape(1, C)), 0)
    gain, shift = inner[0:1], inner[1:2]
    xs[...] = jnp.dot(feat[...], perm[...], preferred_element_type=F32)
    mu = grouped(jnp.sum(xs[...], axis=0, keepdims=True))
    centred = xs[...] - mu
    xs[...] = centred
    inverse = lax.rsqrt(grouped(jnp.sum(centred * centred, axis=0, keepdims=True)) + EPS)

    pl.semaphore_wait(barrier, len(everyone))
    sib_c = rc(cot, scot, SIB, sib)
    sib_c.start()
    def wcols(sc):
        k = jnp.minimum(sc * 8 + lo * 4 + x, 14)
        return w.at[:, pl.ds(pl.multiple_of(k * CH, CH), CH)]

    zc = []
    for dz, dc in zpeers:
        cp = rc(wcols((s + dc) % 2), zbuf.at[z * 2 + s], ZW + dz * 2 + dc, zdev(dz, dc))
        cp.start()
        zc.append(cp)
    own = pltpu.make_async_copy(wcols(s), zbuf.at[z * 2 + s], ss.at[ZW])
    own.start()

    xhat = xs[...] * inverse
    xs[...] = xhat
    pre = xhat * gain + shift
    sg = 1.0 / (1.0 + jnp.exp(-pre))
    ds[...] = sg * (1.0 + pre * (1.0 - sg))
    hid = pre * sg
    hb[...] = hid.astype(BF16)
    ht[:, 0:PIX] = hid.T.astype(BF16)
    def ring_gather(pos, right, left, piece, base):
        rt, lf = (pos + 1) % 4, (pos + 3) % 4
        first_sends = [
            rc(piece(pos, 0), piece(pos, 0), base, right),
            rc(piece(pos, 1), piece(pos, 1), base + 1, left),
            rc(piece(pos, 1), piece(pos, 1), base + 2, right),
            rc(piece(pos, 0), piece(pos, 0), base + 3, left),
        ]
        for cp in first_sends:
            cp.start()

        def relay(arrived):
            first_sends[0].wait_recv()
            f0 = rc(piece(lf, 0), piece(lf, 0), base + 4, right)
            f0.start()
            first_sends[1].wait_recv()
            f1 = rc(piece(rt, 1), piece(rt, 1), base + 5, left)
            f1.start()
            arrived(lf, 0, 1)
            arrived(rt, 1, 2)

            def sides():
                first_sends[2].wait_recv()
                arrived(lf, 1, 1)
                first_sends[3].wait_recv()
                arrived(rt, 0, 2)

            def finish():
                opp = (pos + 2) % 4
                f0.wait_recv()
                arrived(opp, 0, 3)
                f1.wait_recv()
                arrived(opp, 1, 3)
                for cp in first_sends + [f0, f1]:
                    cp.wait_send()
            return sides, finish
        return relay

    def piece_b(j, half):
        return wall.at[s * 16 + ra * 4 + j, pl.ds(half * 160, 160)]

    def piece_a(j, half):
        return wall.at[pl.ds(s * 16 + j * 4 + half * 2, 2)]


    sib_h = rc(ht.at[:, pl.ds(0, PIX)], ht.at[:, pl.ds(PIX, PIX)], SIB + 1, sib)
    sib_h.start()


    sib_c.wait_recv()
    windows(scot, PIX)
    sib_h.wait_recv()

    def chunk(sc, n, late):
        e = 1 - late
        l2 = (1 - sc) * (n % 2) + sc * ((lo + e) % 2)
        xx = (1 - sc) * ((x + e + 2 * (n // 2)) % 4) + sc * n
        return l2 * 4 + xx

    def wgrad(i):
        res = jnp.dot(ht[...], cc[s * 8 + i], preferred_element_type=F32).astype(BF16)
        l2, xx = i // 4, i % 4
        for hh in range(2):
            yy = hh * 2 + l2
            idx = (1 - s) * (xx * 4 + yy) + s * (yy * 4 + xx)
            term[idx] = res[hh * BLK:(hh + 1) * BLK]


    sib_w = {}

    def to_sibling(j, half, rel):
        cp = rc(piece_a(j, half), piece_a(j, half), SW + rel * 2 + half, sib)
        cp.start()
        sib_w[rel, half] = cp

    def ring_reduce(pos, right, left, piece, o, r, base, add, between=lambda: None):
        rt, lf, opp = (pos + 1) % 4, (pos + 3) % 4, (pos + 2) % 4
        sends = [
            rc(piece(opp, 0), o(0), base, right),
            rc(piece(opp, 1), o(1), base + 1, left),
            rc(piece(rt, 1), r(0, 1), base + 2, right),
            rc(piece(lf, 0), r(1, 0), base + 3, left),
        ]
        for cp in sends[:2]:
            cp.start()
        between()
        for cp in sends[2:]:
            cp.start()

        def middle():
            sends[0].wait_recv()
            add(rt, 0)
            g0 = rc(piece(rt, 0), r(0, 0), base + 4, right)
            g0.start()
            sends[1].wait_recv()
            add(lf, 1)
            g1 = rc(piece(lf, 1), r(1, 1), base + 5, left)
            g1.start()

            def finish():
                for cp in (sends[2], sends[3], g0, g1):
                    cp.wait_recv()
                for cp in sends + [g0, g1]:
                    cp.wait_send()
            return finish
        return middle

    def add_a(j, half):
        @pl.loop(0, 2)
        def _(q):
            at = j * 4 + half * 2 + q
            term[at] = (term[at].astype(F32) + o1[half * 2 + q].astype(F32)).astype(BF16)

    pl.loop(0, 4)(lambda n: wgrad(chunk(s, n, 1)))
    middle_ra = ring_reduce(
        ra, a_right, a_left,
        lambda j, half: term.at[pl.ds(j * 4 + half * 2, 2)],
        lambda half: o1.at[pl.ds(half * 2, 2)],
        lambda side, half: r1.at[side, pl.ds(half * 2, 2)],
        RSA, add_a, between=lambda: pl.loop(0, 4)(lambda n: wgrad(chunk(s, n, 0))))

    own.wait()
    for cp in zc:
        cp.wait_recv()
    for q in range(16):
        mf[q * 20:(q + 1) * 20, :] = zbuf[q].astype(F32)
    me = s * 16 + ra * 4 + rb
    wall[me] = mf[...].astype(BF16)

    relay_b = ring_gather(rb, b_right, b_left, piece_b, AGB)
    finish_ra = middle_ra()
    for step in relay_b(lambda j, half, rel: None):
        step()
    relay_a = ring_gather(ra, a_right, a_left, piece_a, AGA)
    to_sibling(ra, 0, 0)
    to_sibling(ra, 1, 0)

    finish_ra()

    def sum_a(j):
        return term[ra * 4 + j].astype(F32) + r1[0, j].astype(F32) + r1[1, j].astype(F32)

    @pl.loop(0, 4)
    def _(j):
        ub[j] = sum_a(j).astype(BF16)

    def add_b(j, half):
        part = pl.ds(half * 160, 160)
        ub[j, part] = (ub[j, part].astype(F32) + o2[half].astype(F32)).astype(BF16)

    middle_rb = ring_reduce(
        rb, b_right, b_left,
        lambda j, half: ub.at[j, pl.ds(half * 160, 160)],
        lambda half: o2.at[half],
        lambda side, half: r2.at[side, pl.ds(half * 160, 160)],
        RSB, add_b)
    sides_a, finish_a = relay_a(to_sibling)
    finish_rb = middle_rb()

    gh[...] = jnp.zeros((PIX, C), F32)

    def block(sc, i):
        l2, xx = i // 4, i % 4
        rows = []
        for hh in range(2):
            yy = hh * 2 + l2
            rows.append(wall[sc * 16 + (1 - sc) * (xx * 4 + yy) + sc * (yy * 4 + xx)])
        return jnp.concatenate(rows, axis=0)

    def back(sc, i):
        gh[...] += lax.dot_general(cc[sc * 8 + i, 0:PIX], block(sc, i), (((1,), (1,)), ((), ())),
                                   preferred_element_type=F32)

    def forth(sc, i):
        pbuf[sc * 8 + i] = jnp.dot(hb[...], block(sc, i), preferred_element_type=F32)

    def loop(f, sc, late):
        pl.loop(0, 4)(lambda n: f(sc, chunk(sc, n, late)))

    def both(sc, i):
        wk = block(sc, i)
        k = sc * 8 + i
        pbuf[k] = jnp.dot(hb[...], wk, preferred_element_type=F32)
        gh[...] += lax.dot_general(cc[k, 0:PIX], wk, (((1,), (1,)), ((), ())),
                                   preferred_element_type=F32)

    finish_rb()
    total = sum_a(rb) + r2[0].astype(F32) + r2[1].astype(F32)
    for q in range(NZ):
        tf[q] = total[q * 40:(q + 1) * 40]
        vb[q] = total[q * 40:(q + 1) * 40].astype(BF16)
    pc = []
    for dz in range(1, NZ):
        cp = rc(vb.at[(z + dz) % NZ], cr.at[z], PC + dz, dev(x, y, (z + dz) % NZ, s))
        cp.start()
        pc.append(cp)
    cr[z] = jnp.zeros((40, CH), BF16)

    sides_a()
    loop(both, s, 0)

    for cp in pc:
        cp.wait_recv()
    full = (jnp.sum(cr[...].astype(F32), axis=0) + tf[z]) / IMAGES
    f2[0] = full[0:20]
    f2[1] = full[20:40]
    slot = s * 8 + lo * 4 + x
    rf[slot] = f2[s]
    fc = []
    for dl, dx, dc in fpeers:
        cp = rc(f2.at[(s + dc) % 2], rf.at[slot], FIN + dl * 8 + dx * 2 + dc, fdev(dl, dx, dc))
        cp.start()
        fc.append(cp)

    for rel, half in ((1, 0), (2, 1), (1, 1), (2, 0)):
        sib_w[rel, half].wait_recv()
    loop(both, 1 - s, 0)
    finish_a()
    loop(back, s, 1)
    for rel, half in ((0, 0), (0, 1), (3, 0), (3, 1)):
        sib_w[rel, half].wait_recv()
    loop(back, 1 - s, 1)

    gp = gh[...] * ds[...]
    gh[...] = gp
    shift_sum = jnp.sum(gp, axis=0, keepdims=True)
    gain_sum = jnp.sum(gp * xs[...], axis=0, keepdims=True)
    for i in range(5):
        vs[0, i:i + 1, :] = gain_sum[:, i * 128:(i + 1) * 128]
        vs[0, 5 + i:6 + i, :] = shift_sum[:, i * 128:(i + 1) * 128]
    v1[z * 2 + s] = vs[0]
    vc = []
    for dz, dc in zpeers:
        cp = rc(vs.at[0], v1.at[z * 2 + s], V1 + dz * 2 + dc, zdev(dz, dc))
        cp.start()
        vc.append(cp)

    m1 = grouped(shift_sum * gain)
    m2 = grouped(gain_sum * gain)
    g = gh[...] * gain
    fgp = ((g - m1 - xs[...] * m2) * inverse).astype(BF16)
    fg[...] = lax.dot_general(fgp, perm[...], (((1,), (1,)), ((), ())),
                              preferred_element_type=F32).astype(BF16)

    for cp in vc:
        cp.wait_recv()
    vs[1] = jnp.sum(v1[...], axis=0)
    v2[x] = vs[1]
    vx = []
    for k in (1, 2, 3):
        cp = rc(vs.at[1], v2.at[x], V2 + k, dev((x + k) % 4, y, z, s))
        cp.start()
        vx.append(cp)
    loop(forth, s, 1)
    for cp in vx:
        cp.wait_recv()
    vs[2] = jnp.sum(v2[...], axis=0)
    v3[y] = vs[2]
    vy = []
    for k in (1, 2, 3):
        cp = rc(vs.at[2], v3.at[y], V3 + k, dev(x, (y + k) % 4, z, s))
        cp.start()
        vy.append(cp)
    loop(forth, 1 - s, 1)

    for ot in range(5):
        total = None
        for b in range(3):
            parts = []
            for a in range(3):
                k, i = divmod(5 * (3 * a + b) + ot, 3)
                p = pbuf[k, :, i * 128:(i + 1) * 128]
                pad = jnp.zeros((SIDE, 128), F32)
                if a == 0:
                    p = jnp.concatenate([pad, p[:PIX - SIDE]], axis=0)
                elif a == 2:
                    p = jnp.concatenate([p[SIDE:], pad], axis=0)
                parts.append(p)
            sb = parts[0] + parts[1] + parts[2]
            if b == 0:
                sb = jnp.where(first[:, :128], 0.0, pltpu.roll(sb, 1, 0))
            elif b == 2:
                sb = jnp.where(last[:, :128], 0.0, pltpu.roll(sb, PIX - 1, 0))
            total = sb if total is None else total + sb
        cols = slice(ot * 128, (ot + 1) * 128)
        out[:, cols] = (total + bias[:, cols]).astype(BF16)

    for cp in fc:
        cp.wait_recv()
    for k in range(15):
        wg[:, k * CH:(k + 1) * CH] = rf[k]
    for cp in vy:
        cp.wait_recv()
    sums = jnp.sum(v3[...], axis=0) / IMAGES
    vo[...] = jnp.zeros((8, C), F32)
    for q in range(3):
        for i in range(5):
            vo[q:q + 1, i * 128:(i + 1) * 128] = sums[q * 5 + i:q * 5 + i + 1]
    outer = moved(vo[...], 1)
    out_gain[...] = outer[0:1].reshape(C)
    out_shift[...] = outer[1:2].reshape(C)
    out_bias[...] = vo[2:3].reshape(C)
    for cp in zc + [sib_c, sib_h] + list(sib_w.values()) + vc + vx + vy + pc + fc:
        cp.wait_send()


def put_out(*refs):
    sems = refs[12]
    copies = [pltpu.make_async_copy(refs[i], refs[6 + i], sems.at[i]) for i in range(6)]
    for cp in copies:
        cp.start()
    for cp in copies:
        cp.wait()


def local(features, weight, gain, shift, bias, cotangent):
    order = np.arange(C).reshape(NZ, 2, GROUP).transpose(1, 0, 2).reshape(C)
    perm = np.zeros((C, C), np.float32)
    perm[order, np.arange(C)] = 1.0
    ind = np.zeros((C, 128), np.float32)
    ind[np.arange(C), np.arange(C) // GROUP] = 1.0
    vm = pl.BlockSpec(memory_space=pltpu.VMEM)
    held = pl.pallas_call(
        kernel,
        name="fused_step",
        out_shape=[
            pltpu.VMEM((PIX, C), BF16),
            pltpu.VMEM((PIX, C), BF16),
            pltpu.VMEM((20, 9 * C), F32),
            pltpu.VMEM((C,), F32),
            pltpu.VMEM((C,), F32),
            pltpu.VMEM((C,), F32),
        ],
        in_specs=[pl.BlockSpec(memory_space=pl.ANY)] * 9,
        out_specs=[vm] * 6,
        scratch_shapes=[
            pltpu.VMEM((16, 20, CH), BF16),
            pltpu.VMEM((BLK, CH), F32),
            pltpu.VMEM((32, BLK, CH), BF16),
            pltpu.VMEM((16, BLK, CH), BF16),
            pltpu.VMEM((PIX, C), F32),
            pltpu.VMEM((PIX, C), F32),
            pltpu.VMEM((PIX, C), BF16),
            pltpu.VMEM((C, 2 * PIX), BF16),
            pltpu.VMEM((16, 2 * PIX, CH), BF16),
            pltpu.VMEM((3, PIX + 2 * SIDE, C), BF16),
            pltpu.VMEM((16, PIX, CH), F32),
            pltpu.VMEM((PIX, C), F32),
            pltpu.VMEM((4, BLK, CH), BF16),
            pltpu.VMEM((2, 4, BLK, CH), BF16),
            pltpu.VMEM((4, BLK, CH), BF16),
            pltpu.VMEM((2, 160, CH), BF16),
            pltpu.VMEM((2, BLK, CH), BF16),
            pltpu.VMEM((NZ, 40, CH), BF16),
            pltpu.VMEM((NZ, 40, CH), BF16),
            pltpu.VMEM((NZ, 40, CH), F32),
            pltpu.VMEM((2, 20, CH), F32),
            pltpu.VMEM((16, 20, CH), F32),
            pltpu.VMEM((3, 16, 128), F32),
            pltpu.VMEM((16, 16, 128), F32),
            pltpu.VMEM((4, 16, 128), F32),
            pltpu.VMEM((4, 16, 128), F32),
            pltpu.VMEM((PIX, C), BF16),
            pltpu.VMEM((8, C), F32),
            pltpu.VMEM((PIX, C), BF16),
            pltpu.VMEM((20, 9 * C), BF16),
            pltpu.VMEM((C,), F32),
            pltpu.VMEM((C,), F32),
            pltpu.VMEM((C,), F32),
            pltpu.VMEM((PIX, C), BF16),
            pltpu.VMEM((C, C), BF16),
            pltpu.VMEM((C, 128), F32),
            pltpu.VMEM((128, C), F32),
            pltpu.SemaphoreType.DMA((9,)),
            pltpu.SemaphoreType.DMA((NSEM,)),
            pltpu.SemaphoreType.DMA((NSEM,)),
        ],
        compiler_params=pltpu.CompilerParams(
            collective_id=0, has_side_effects=True, vmem_limit_bytes=60 * 1024 * 1024),
    )(features.reshape(PIX, C), weight, gain, shift, bias, cotangent.reshape(PIX, C),
      jnp.asarray(perm, BF16), jnp.asarray(ind), jnp.asarray(ind.T.copy()))
    shape = features.shape
    out, fg, wg, g_gain, g_shift, g_bias = pl.pallas_call(
        put_out,
        name="put_out",
        out_shape=[jax.ShapeDtypeStruct(v.shape, v.dtype) for v in held],
        in_specs=[vm] * 6,
        out_specs=[pl.BlockSpec(memory_space=pl.ANY)] * 6,
        scratch_shapes=[pltpu.SemaphoreType.DMA((6,))],
        compiler_params=pltpu.CompilerParams(vmem_limit_bytes=8 * 1024 * 1024),
    )(*held)
    return out.reshape(shape), fg.reshape(shape), wg, g_gain, g_shift, g_bias


def solution(mesh):
    img = P(("fsdp", "dp"), None, None, None)
    return jax.shard_map(
        local, mesh=mesh,
        in_specs=(img, P("fsdp", None), P(), P(), P(), img),
        out_specs=(img, img, P("fsdp", None), P(), P(), P()),
        check_vma=False)
```
